32 devices in a mesh: task: 8 (over z, x), own: 4 (over y, core).
Axes of the slice: x: 2, y: 2, z: 4, core: 2. Of those that a mesh axis runs over, the one named last changes fastest.
Arguments:
- amplitudes: bfloat16 [64, 384, 128], P(('task', 'own')), may hold values from -6 to 6
- integrals: bfloat16 [2048, 128, 128], P(('task', 'own')), may hold values from -0.125 to 0.125
- task_tiles: int32 [2048, 3], P(('task', 'own')), may hold values from 0 to 7, as said below
- task_count: int32 [32], P(('task', 'own')), may hold values from 8 to 64, as said below
Outputs:
- residual: float32 [64, 384, 128], P(('task', 'own'))
The draws below stay inside these ranges and needn't reach their ends.
Inputs may be any that keep to these rules, and one draw needn't show every extreme that they name: `task_tiles`: column 0 is 0 or 1, columns 1 and 2 are tiles of a group, below 8. Among the slots of one executor, the target tiles t with t // 2 = o number exactly 16 for every o below 4. `task_count`: in every task group one executor has all 64 slots live.
All inputs are finite; a program needn't handle non-finite values.
Results may differ from the reference program's by a relative error of at most 0.0003.
Values may be sent and summed in bfloat16 or wider, within the bound.
A program may use at most 64 MiB of HBM per device.

```python
import jax
import jax.numpy as jnp
from jax import lax

TILE = 128
OCC_PAIRS = 384
TILES_DEV = 2
TASKS_DEV = 64
OWNERS = 4
GROUPS = 8
GROUP_TILES = 8
NT = 64
NK = 2048
EXECUTORS = 32


def draw_task_tiles(key, part):
    keys = jax.random.split(jax.random.fold_in(key, 11), 4)
    offset = jax.random.randint(keys[0], (NK,), 0, 2)
    source = jax.random.randint(keys[1], (NK,), 0, GROUP_TILES)
    base = jnp.repeat(jnp.arange(OWNERS, dtype=jnp.int32), TASKS_DEV // OWNERS)
    shuffle_keys = jax.random.split(keys[2], EXECUTORS)
    owners_of = jax.vmap(lambda k: jax.random.permutation(k, base))(shuffle_keys).reshape(NK)
    within = jax.random.randint(keys[3], (NK,), 0, TILES_DEV)
    target = owners_of * TILES_DEV + within
    return jnp.stack([offset, source, target], 1).astype(jnp.int32)


def draw_task_count(key, part):
    keys = jax.random.split(jax.random.fold_in(key, 23), 2)
    counts = jax.random.randint(keys[0], (EXECUTORS,), TASKS_DEV // 8, TASKS_DEV // 2 + 1)
    fullest = jax.random.randint(keys[1], (GROUPS,), 0, OWNERS)
    where_full = jnp.arange(GROUPS, dtype=jnp.int32) * OWNERS + fullest
    return counts.at[where_full].set(TASKS_DEV).astype(jnp.int32)


def shard_levels(own_key, shape, cuts, smallest, largest):
    factor_of, own = 1.0, jax.random.fold_in(own_key, 6)
    for position, blocks in cuts:
        heights = jnp.exp(jax.random.uniform(jax.random.fold_in(own, position), (blocks,), jnp.float32, smallest / len(cuts), largest / len(cuts)))
        factor_of = factor_of * jnp.repeat(heights, shape[position] // blocks).reshape([-1 if axis == position else 1 for axis in range(len(shape))])
    return factor_of


def centred(key, dims, scale, bound, cuts=(), kind=jnp.bfloat16):
    values = jax.random.normal(key, dims, jnp.float32) * scale
    if len(cuts) > 0:
        values = shard_levels(key, dims, cuts, -0.22, 0.18) * values
    return jnp.clip(values, min=-bound, max=bound).astype(kind)


def setup_inputs(seed: int = 0) -> dict:
    seeds = jax.random.split(jax.random.key(seed), 5)
    return {
        "amplitudes": centred(seeds[0], (NT, OCC_PAIRS, TILE), 1.0, 6.0, ((0, 32),)),
        "integrals": centred(seeds[1], (NK, TILE, TILE), (TILE * 16) ** -0.5, 0.125, ((0, 32),)),
        "task_tiles": draw_task_tiles(jax.random.fold_in(seeds[4], 71), 0),
        "task_count": draw_task_count(jax.random.fold_in(seeds[4], 71), 0),
    }


def reference(amplitudes, integrals, task_tiles, task_count):
    slots = jnp.arange(TASKS_DEV, dtype=jnp.int32)

    def one_executor(total, executor):
        group = executor // OWNERS
        begin = (executor * TASKS_DEV).astype(jnp.int32)
        blocks = lax.dynamic_slice_in_dim(integrals, begin, TASKS_DEV, 0).astype(jnp.float32)
        lists = lax.dynamic_slice_in_dim(task_tiles, begin, TASKS_DEV, 0)
        live = (slots < task_count[executor]).astype(jnp.float32)
        source = (((group - lists[:, 0]) % GROUPS) * GROUP_TILES + lists[:, 1]).astype(jnp.int32)
        target = (group * GROUP_TILES + lists[:, 2]).astype(jnp.int32)
        tiles = amplitudes[source].astype(jnp.float32)
        product = jnp.einsum("kic,kcr->kir", tiles, blocks, precision=lax.Precision.HIGHEST)
        product = product * live[:, None, None]
        return total.at[target].add(product), None

    start = jnp.zeros((NT, OCC_PAIRS, TILE), jnp.float32)
    total, unused = lax.scan(one_executor, start, jnp.arange(EXECUTORS, dtype=jnp.int32))
    return total
```

```python
import functools

import jax
import jax.numpy as jnp
from jax import lax
from jax.experimental import pallas as pl
from jax.experimental.pallas import tpu as pltpu
from jax.sharding import PartitionSpec as P

MESH = pl.DeviceIdType.MESH
CHUNKS = 3
AHEAD = 2
LEVELS = 32767.0
TINY = 1e-33
VMEM_BYTES = 48 * 2**20


def kernel(dims, amp, integ, lists_hbm, count, out, *scratch):
    groups, n, tiles, slots, rows_all, width = dims
    half = n // 2
    per_owner = slots // n
    rows = rows_all // CHUNKS
    wide = tiles * width
    group_tiles = n * tiles
    gath = scratch[:CHUNKS]
    (vbuf, weights, psend, precv, pown, qsend, qrecv, ssend, srecv, lists, following, source,
     local_sem, v_sem, list_sem, sy, ry, sn, rn, ss, rs, st, rt, sp, rp, sq, rq, sc, rc) = scratch[CHUNKS:]

    g = lax.axis_index("task")
    me = lax.axis_index("own")
    core = lax.rem(me, 2)
    y = lax.div(me, 2)
    next_g = lax.rem(g + 1, groups)
    prev_g = lax.rem(g + groups - 1, groups)
    sibling = y * 2 + 1 - core
    to_sibling = {"task": g, "own": sibling}
    to_next = {"task": next_g, "own": me}

    def ahead(d):
        return lax.rem(y + d, half) * 2 + core

    def behind(d):
        return lax.rem(y + half - d, half) * 2 + core

    list_copy = pltpu.make_async_copy(lists_hbm, lists, list_sem)
    list_copy.start()
    barrier = pltpu.get_barrier_semaphore()
    for d in range(1, half):
        pl.semaphore_signal(barrier, inc=1, device_id={"task": g, "own": ahead(d)}, device_id_type=MESH)
    pl.semaphore_signal(barrier, inc=1, device_id=to_sibling, device_id_type=MESH)
    pl.semaphore_signal(barrier, inc=1, device_id={"task": prev_g, "own": me}, device_id_type=MESH)

    v_copy = pltpu.make_async_copy(integ, vbuf, v_sem)
    v_copy.start()
    local = []

    def own_rows(c):
        return amp.at[:, pl.ds(c * rows, rows), :]

    def slot(c, offset, owner):
        return gath[c].at[pl.ds((offset * n + owner) * tiles, tiles)]

    for c in range(CHUNKS):
        copy = pltpu.make_async_copy(own_rows(c), slot(c, 0, me), local_sem.at[c])
        copy.start()
        local.append(copy)

    sends = []

    def remote(src, dst, send_sem, recv_sem, device):
        copy = pltpu.make_async_remote_copy(
            src_ref=src, dst_ref=dst, send_sem=send_sem, recv_sem=recv_sem, device_id=device, device_id_type=MESH
        )
        copy.start()
        sends.append(copy)

    def arrived(dst, recv_sem):
        pltpu.make_async_copy(dst, dst, recv_sem).wait()

    pl.semaphore_wait(barrier, half + 1)

    def send_y(c):
        for d in range(1, half):
            remote(own_rows(c), slot(c, 0, me), sy.at[c, d - 1], ry.at[c, d - 1], {"task": g, "own": ahead(d)})

    def send_next(c):
        remote(own_rows(c), slot(c, 1, me), sn.at[c, 0], rn.at[c, 0], to_next)

    def send_sibling(c):
        remote(own_rows(c), slot(c, 0, me), ss.at[c, 0], rs.at[c, 0], to_sibling)

    for c in range(CHUNKS):
        send_y(c)
        if c < AHEAD:
            send_next(c)
        send_sibling(c)

    def relay_y(c):
        for d in range(1, half):
            here = slot(c, 0, behind(d))
            arrived(here, ry.at[c, d - 1])
            remote(here, slot(c, 1, behind(d)), sn.at[c, d], rn.at[c, d], to_next)
            remote(here, slot(c, 0, behind(d)), ss.at[c, d], rs.at[c, d], to_sibling)
        if c + AHEAD < CHUNKS:
            send_next(c + AHEAD)

    def relay_next(c):
        for d in range(half):
            here = slot(c, 1, behind(d))
            arrived(here, rn.at[c, d])
            remote(here, slot(c, 1, behind(d)), st.at[c, d], rt.at[c, d], to_sibling)

    list_copy.wait()
    for o in range(n):
        following[slots * n + o] = 0

    def back(step, firsts):
        k = slots - 1 - step
        owner = lax.div(lists[2, k], tiles)
        fresh = []
        for o in range(n):
            first = jnp.where(owner == o, k, firsts[o])
            following[k * n + o] = first
            fresh.append(first)
        return tuple(fresh)

    lax.fori_loop(0, slots, back, tuple(jnp.int32(0) for _ in range(n)))
    v_copy.wait()
    live_slots = count[0]

    def weigh(o, carry):
        k = following[o]
        for j in range(per_owner):
            block = vbuf[k]
            target = lax.rem(lists[2, k], tiles)
            source[o * per_owner + j] = lists[0, k] * group_tiles + lists[1, k]
            for t in range(tiles):
                keep = jnp.logical_and(target == t, k < live_slots)
                weights[o, j * width:(j + 1) * width, t * width:(t + 1) * width] = jnp.where(
                    keep, block, jnp.zeros_like(block)
                )
            k = following[(k + 1) * n + o]
        return carry

    lax.fori_loop(0, n, weigh, 0)

    def product(c, o):
        total = jnp.zeros((rows, wide), jnp.float32)
        for j in range(0, per_owner, 2):
            left = gath[c][source[o * per_owner + j]]
            right = gath[c][source[o * per_owner + j + 1]]
            total = total + jnp.dot(
                jnp.concatenate([left, right], -1),
                weights[o, j * width:(j + 2) * width, :],
                preferred_element_type=jnp.float32,
            )
        return total

    def compute(c):
        local[c].wait()
        for d in range(half):
            other = lax.rem(y + half - d, half) * 2 + 1 - core
            arrived(slot(c, 0, other), rs.at[c, d])
            arrived(slot(c, 1, other), rt.at[c, d])
        for d in range(half):
            psend[c, d] = product(c, lax.rem(y + d + 1, half) * 2 + 1 - core)
            remote(psend.at[c, d], precv.at[c, d], sp.at[c, d], rp.at[c, d], to_sibling)
        for d in range(half):
            pown[c, d] = product(c, lax.rem(y + d + 1, half) * 2 + core)

    def exchange(c):
        for d in range(half - 1):
            arrived(precv.at[c, d], rp.at[c, d])
            total = pown[c, d] + precv[c, d]
            top = jnp.maximum(jnp.max(jnp.abs(total), axis=0, keepdims=True), TINY)
            qsend[c, d] = jnp.round(total * (LEVELS / top)).astype(jnp.int32).astype(jnp.int16)
            ssend[c, d] = jnp.broadcast_to(top * (1.0 / LEVELS), (8, wide))
            device = {"task": g, "own": ahead(d + 1)}
            remote(qsend.at[c, d], qrecv.at[c, d], sq.at[c, d], rq.at[c, d], device)
            remote(ssend.at[c, d], srecv.at[c, d], sc.at[c, d], rc.at[c, d], device)

    def finish(c):
        arrived(precv.at[c, half - 1], rp.at[c, half - 1])
        total = pown[c, half - 1] + precv[c, half - 1]
        for d in range(half - 1):
            arrived(qrecv.at[c, d], rq.at[c, d])
            arrived(srecv.at[c, d], rc.at[c, d])
            total = total + qrecv[c, d].astype(jnp.int32).astype(jnp.float32) * srecv[c, d][0:1]
        for t in range(tiles):
            out[t, c * rows:(c + 1) * rows, :] = total[:, t * width:(t + 1) * width]

    stages = (relay_y, relay_next, compute, exchange, finish)
    for step in range(CHUNKS + len(stages) - 1):
        for late, stage in enumerate(stages):
            if 0 <= step - late < CHUNKS:
                stage(step - late)
    for copy in sends:
        copy.wait_send()


def shards(amplitudes, integrals, task_tiles, task_count):
    tiles, rows_all, width = amplitudes.shape
    slots = integrals.shape[0]
    groups, n = lax.axis_size("task"), lax.axis_size("own")
    half = n // 2
    rows = rows_all // CHUNKS
    wide = tiles * width
    dma = pltpu.SemaphoreType.DMA
    peers = half - 1
    scratch = [pltpu.VMEM((2 * n * tiles, rows, width), amplitudes.dtype) for _ in range(CHUNKS)]
    scratch += [
        pltpu.VMEM(integrals.shape, integrals.dtype),
        pltpu.VMEM((n, slots // n * width, wide), integrals.dtype),
        pltpu.VMEM((CHUNKS, half, rows, wide), jnp.float32),
        pltpu.VMEM((CHUNKS, half, rows, wide), jnp.float32),
        pltpu.VMEM((CHUNKS, half, rows, wide), jnp.float32),
        pltpu.VMEM((CHUNKS, peers, rows, wide), jnp.int16),
        pltpu.VMEM((CHUNKS, peers, rows, wide), jnp.int16),
        pltpu.VMEM((CHUNKS, peers, 8, wide), jnp.float32),
        pltpu.VMEM((CHUNKS, peers, 8, wide), jnp.float32),
        pltpu.SMEM((3, slots), jnp.int32),
        pltpu.SMEM(((slots + 1) * n,), jnp.int32),
        pltpu.SMEM((slots,), jnp.int32),
        dma((CHUNKS,)),
        dma,
        dma,
        dma((CHUNKS, peers)), dma((CHUNKS, peers)),
        dma((CHUNKS, half)), dma((CHUNKS, half)),
        dma((CHUNKS, half)), dma((CHUNKS, half)),
        dma((CHUNKS, half)), dma((CHUNKS, half)),
        dma((CHUNKS, half)), dma((CHUNKS, half)),
        dma((CHUNKS, peers)), dma((CHUNKS, peers)),
        dma((CHUNKS, peers)), dma((CHUNKS, peers)),
    ]
    dims = (groups, n, tiles, slots, rows_all, width)
    held = [pltpu.with_memory_space_constraint(x, pltpu.HBM) for x in (amplitudes, integrals, task_tiles.T)]
    return pl.pallas_call(
        functools.partial(kernel, dims),
        out_shape=pltpu.VMEM((tiles, rows_all, width), jnp.float32),
        in_specs=[
            pl.BlockSpec(memory_space=pl.ANY),
            pl.BlockSpec(memory_space=pl.ANY),
            pl.BlockSpec(memory_space=pl.ANY),
            pl.BlockSpec(memory_space=pltpu.SMEM),
        ],
        out_specs=pl.BlockSpec(memory_space=pltpu.VMEM),
        scratch_shapes=scratch,
        compiler_params=pltpu.CompilerParams(collective_id=0, has_side_effects=True, vmem_limit_bytes=VMEM_BYTES),
        name="ladder",
    )(*held, task_count)


def solution(mesh):
    return jax.shard_map(
        shards,
        mesh=mesh,
        in_specs=(
            P(("task", "own"), None, None),
            P(("task", "own"), None, None),
            P(("task", "own"), None),
            P(("task", "own")),
        ),
        out_specs=P(("task", "own"), None, None),
        check_vma=False,
    )
```

```python
import functools

import jax
import jax.numpy as jnp
from jax import lax
from jax.experimental import pallas as pl
from jax.experimental.pallas import tpu as pltpu
from jax.sharding import PartitionSpec as P

MESH = pl.DeviceIdType.MESH
CHUNKS = 3
ACROSS = (2,)
ORDER_Y = (2, 0, 1)
ORDER_NEXT = (0, 1, 2)
LEVELS = 32767.0
TINY = 1e-33
VMEM_BYTES = 48 * 2**20


def messages(half):
    keys = [("integrals",), ("lists",), ("count",), ("partial",)]
    for c in range(CHUNKS):
        keys += [("sibling", c), ("next", c, 0), ("next", c, 1)]
        for d in range(1, half):
            keys += [("y", c, d, 0), ("y", c, d, 1), ("relay", c, d)]
            keys += [("sum", c, d, 0), ("sum", c, d, 1), ("scale", c, d, 0), ("scale", c, d, 1)]
    return {key: i for i, key in enumerate(keys)}


def kernel(dims, amp, integ, lists_hbm, count, out, *scratch):
    groups, n, tiles, slots, rows_all, width = dims
    half = n // 2
    per_owner = slots // n
    rows_core = rows_all // 2
    rows = rows_core // CHUNKS
    wide = tiles * width
    group_tiles = n * tiles
    index = messages(half)
    gath = scratch[:CHUNKS]
    (v_own, v_sib, weights, mine, psend, precv, qsend, qrecv, ssend, srecv, lists, lists_sib, count_sib, following, source,
     local_sem, send_sem, recv_sem) = scratch[CHUNKS:]

    g = lax.axis_index("task")
    me = lax.axis_index("own")
    core = lax.rem(me, 2)
    y = lax.div(me, 2)
    other = 1 - core
    next_g = lax.rem(g + 1, groups)
    prev_g = lax.rem(g + groups - 1, groups)
    sibling = y * 2 + other

    def ahead(d):
        return lax.rem(y + d, half)

    def behind(d):
        return lax.rem(y + half - d, half)

    def device(owner, group=g):
        return {"task": group, "own": owner}

    list_copy = pltpu.make_async_copy(lists_hbm, lists, local_sem.at[CHUNKS])
    list_copy.start()
    barrier = pltpu.get_barrier_semaphore()
    for owner in (me, sibling):
        pl.semaphore_signal(barrier, inc=1, device_id=device(owner, prev_g), device_id_type=MESH)
    for d in range(1, half):
        for rel in (core, other):
            pl.semaphore_signal(barrier, inc=1, device_id=device(ahead(d) * 2 + rel), device_id_type=MESH)
    pl.semaphore_signal(barrier, inc=1, device_id=device(sibling), device_id_type=MESH)
    v_copy = pltpu.make_async_copy(integ, v_own, local_sem.at[CHUNKS + 1])
    v_copy.start()

    def own_rows(c, part):
        return amp.at[:, pl.ds(pl.multiple_of(part * rows_core + c * rows, 16), rows), :]

    def slot(c, offset, owner, count=1):
        return gath[c].at[pl.ds((offset * n + owner) * tiles, count * tiles)]

    local = []
    for c in range(CHUNKS):
        copy = pltpu.make_async_copy(own_rows(c, core), slot(c, 0, me), local_sem.at[c])
        copy.start()
        local.append(copy)

    sends = []

    def remote(key, src, dst, target):
        i = index[key]
        copy = pltpu.make_async_remote_copy(
            src_ref=src, dst_ref=dst, send_sem=send_sem.at[i], recv_sem=recv_sem.at[i], device_id=target, device_id_type=MESH
        )
        copy.start()
        sends.append(copy)

    def arrived(key, dst):
        pltpu.make_async_copy(dst, dst, recv_sem.at[index[key]]).wait()

    pl.semaphore_wait(barrier, n + 1)

    for step in range(CHUNKS):
        c = ORDER_NEXT[step]
        remote(("next", c, 0), own_rows(c, core), slot(c, 1, me), device(me, next_g))
        remote(("next", c, 1), own_rows(c, other), slot(c, 1, me), device(sibling, next_g))
        c = ORDER_Y[step]
        for d in range(1, half):
            remote(("y", c, d, 0), own_rows(c, core), slot(c, 0, me), device(ahead(d) * 2 + core))
            remote(("y", c, d, 1), own_rows(c, other), slot(c, 0, me), device(ahead(d) * 2 + other))
        if step == 0:
            remote(("lists",), lists_hbm, lists_sib, device(sibling))
            remote(("count",), count, count_sib, device(sibling))
            remote(("integrals",), integ, v_sib, device(sibling))
    for c in range(CHUNKS):
        remote(("sibling", c), own_rows(c, other), slot(c, 0, me), device(sibling))

    list_copy.wait()
    arrived(("lists",), lists_sib)
    arrived(("count",), count_sib)
    both = ((lists, count, v_own), (lists_sib, count_sib, v_sib))
    span = (slots + 1) * n
    for e in range(2):
        for o in range(n):
            following[e * span + slots * n + o] = 0

    def back(step, firsts):
        k = slots - 1 - step
        fresh = []
        for e in range(2):
            owner = lax.div(both[e][0][2, k], tiles)
            for o in range(n):
                first = jnp.where(owner == o, k, firsts[e * n + o])
                following[e * span + k * n + o] = first
                fresh.append(first)
        return tuple(fresh)

    lax.fori_loop(0, slots, back, tuple(jnp.int32(0) for _ in range(2 * n)))

    def weigh_all(e):
        names, live, blocks = both[e]
        live_slots = live[0]

        def weigh(o, carry):
            k = following[e * span + o]
            for j in range(per_owner):
                block = blocks[k]
                target = lax.rem(names[2, k], tiles)
                place = e * per_owner + j
                source[o * 2 * per_owner + place] = names[0, k] * group_tiles + names[1, k]
                for t in range(tiles):
                    keep = jnp.logical_and(target == t, k < live_slots)
                    weights[o, place * width:(place + 1) * width, t * width:(t + 1) * width] = jnp.where(
                        keep, block, jnp.zeros_like(block)
                    )
                k = following[e * span + (k + 1) * n + o]
            return carry

        lax.fori_loop(0, n, weigh, 0)

    def product(chunks, o):
        total = jnp.zeros((rows * len(chunks), wide), jnp.float32)
        for j in range(0, 2 * per_owner, 2):
            left = source[o * 2 * per_owner + j]
            right = source[o * 2 * per_owner + j + 1]
            tall = [jnp.concatenate([gath[c][left], gath[c][right]], -1) for c in chunks]
            total = total + jnp.dot(
                jnp.concatenate(tall, 0) if len(tall) > 1 else tall[0],
                weights[o, j * width:(j + 2) * width, :],
                preferred_element_type=jnp.float32,
            )
        return total

    def relay_next(c):
        for d in range(1, half):
            here = slot(c, 0, behind(d) * 2, 2)
            arrived(("y", c, d, 0), slot(c, 0, behind(d) * 2 + core))
            arrived(("y", c, d, 1), slot(c, 0, behind(d) * 2 + other))
            remote(("relay", c, d), here, slot(c, 1, behind(d) * 2, 2), device(me, next_g))

    def relay_y(c):
        arrived(("next", c, 0), slot(c, 1, me))
        arrived(("next", c, 1), slot(c, 1, sibling))
        for d in range(1, half):
            here = slot(c, 1, y * 2, 2)
            remote(("relay", c, d), here, here, device(ahead(d) * 2 + core))

    def gathered(c):
        local[c].wait()
        arrived(("sibling", c), slot(c, 0, sibling))
        if c in ACROSS:
            arrived(("next", c, 0), slot(c, 1, me))
            arrived(("next", c, 1), slot(c, 1, sibling))
        else:
            for d in range(1, half):
                arrived(("y", c, d, 0), slot(c, 0, behind(d) * 2 + core))
                arrived(("y", c, d, 1), slot(c, 0, behind(d) * 2 + other))
        for d in range(1, half):
            arrived(("relay", c, d), slot(c, 1, behind(d) * 2, 2))

    def send_sums(c):
        for d in range(1, half):
            for rel, side in enumerate((core, other)):
                o = ahead(d) * 2 + side
                total = product([c], o)
                top = jnp.maximum(jnp.max(jnp.abs(total), axis=0, keepdims=True), TINY)
                qsend[c, d - 1, rel] = jnp.round(total * (LEVELS / top)).astype(jnp.int32).astype(jnp.int16)
                ssend[c, d - 1, rel] = top * (1.0 / LEVELS)
                remote(("sum", c, d, rel), qsend.at[c, d - 1, rel], qrecv.at[c, d - 1, rel], device(o))
                remote(("scale", c, d, rel), ssend.at[c, d - 1, rel], srecv.at[c, d - 1, rel], device(o))

    def finish(c, rel):
        part = pl.ds(c * rows, rows)
        total = (mine if rel == 0 else precv)[part]
        for d in range(1, half):
            arrived(("sum", c, d, rel), qrecv.at[c, d - 1, rel])
            arrived(("scale", c, d, rel), srecv.at[c, d - 1, rel])
            total = total + qrecv[c, d - 1, rel].astype(jnp.int32).astype(jnp.float32) * srecv[c, d - 1, rel]
        first = pl.multiple_of((core if rel == 0 else other) * rows_core + c * rows, 8)
        for t in range(tiles):
            out[t, pl.ds(first, rows), :] = total[:, t * width:(t + 1) * width]

    v_copy.wait()
    weigh_all(0)
    arrived(("integrals",), v_sib)
    weigh_all(1)
    for c in ACROSS:
        relay_next(c)
    for c in range(CHUNKS):
        if c not in ACROSS:
            relay_y(c)
    for c in range(CHUNKS):
        gathered(c)
        send_sums(c)
    every = list(range(CHUNKS))
    psend[...] = product(every, sibling)
    remote(("partial",), psend, precv, device(sibling))
    mine[...] = product(every, me)
    for c in range(CHUNKS):
        finish(c, 0)
    arrived(("partial",), precv)
    for c in range(CHUNKS):
        finish(c, 1)
    for copy in sends:
        copy.wait_send()


def shards(amplitudes, integrals, task_tiles, task_count):
    tiles, rows_all, width = amplitudes.shape
    slots = integrals.shape[0]
    groups, n = lax.axis_size("task"), lax.axis_size("own")
    half = n // 2
    peers = half - 1
    rows_core = rows_all // 2
    rows = rows_core // CHUNKS
    wide = tiles * width
    total = len(messages(half))
    dma = pltpu.SemaphoreType.DMA
    scratch = [pltpu.VMEM((2 * n * tiles, rows, width), amplitudes.dtype) for _ in range(CHUNKS)]
    scratch += [
        pltpu.VMEM(integrals.shape, integrals.dtype),
        pltpu.VMEM(integrals.shape, integrals.dtype),
        pltpu.VMEM((n, 2 * slots // n * width, wide), integrals.dtype),
        pltpu.VMEM((rows_core, wide), jnp.float32),
        pltpu.VMEM((rows_core, wide), jnp.float32),
        pltpu.VMEM((rows_core, wide), jnp.float32),
        pltpu.VMEM((CHUNKS, peers, 2, rows, wide), jnp.int16),
        pltpu.VMEM((CHUNKS, peers, 2, rows, wide), jnp.int16),
        pltpu.VMEM((CHUNKS, peers, 2, 1, wide), jnp.float32),
        pltpu.VMEM((CHUNKS, peers, 2, 1, wide), jnp.float32),
        pltpu.SMEM((3, slots), jnp.int32),
        pltpu.SMEM((3, slots), jnp.int32),
        pltpu.SMEM((1,), jnp.int32),
        pltpu.SMEM((2 * (slots + 1) * n,), jnp.int32),
        pltpu.SMEM((2 * slots,), jnp.int32),
        dma((CHUNKS + 2,)),
        dma((total,)),
        dma((total,)),
    ]
    dims = (groups, n, tiles, slots, rows_all, width)
    held = [pltpu.with_memory_space_constraint(x, pltpu.HBM) for x in (amplitudes, integrals, task_tiles.T)]
    return pl.pallas_call(
        functools.partial(kernel, dims),
        out_shape=pltpu.VMEM((tiles, rows_all, width), jnp.float32),
        in_specs=[
            pl.BlockSpec(memory_space=pl.ANY),
            pl.BlockSpec(memory_space=pl.ANY),
            pl.BlockSpec(memory_space=pl.ANY),
            pl.BlockSpec(memory_space=pltpu.SMEM),
        ],
        out_specs=pl.BlockSpec(memory_space=pltpu.VMEM),
        scratch_shapes=scratch,
        compiler_params=pltpu.CompilerParams(collective_id=0, has_side_effects=True, vmem_limit_bytes=VMEM_BYTES),
        name="ladder",
    )(*held, task_count)


def solution(mesh):
    return jax.shard_map(
        shards,
        mesh=mesh,
        in_specs=(
            P(("task", "own"), None, None),
            P(("task", "own"), None, None),
            P(("task", "own"), None),
            P(("task", "own")),
        ),
        out_specs=P(("task", "own"), None, None),
        check_vma=False,
    )
```

```python
import functools

import jax
import jax.numpy as jnp
from jax import lax
from jax.experimental import pallas as pl
from jax.experimental.pallas import tpu as pltpu
from jax.sharding import PartitionSpec as P

MESH = pl.DeviceIdType.MESH
CHUNKS = 6
ROUTES = "yyyyxx"
ORDER_Y = (4, 5, 0, 1, 2, 3)
ORDER_NEXT = (0, 1, 2, 3, 4, 5)
SETS = ((0,), (1, 4), (2, 3, 5))
LEVELS = 32767.0
TINY = 1e-33
VMEM_BYTES = 48 * 2**20


def messages(half):
    keys = [("integrals",), ("lists",), ("count",), ("partial",)]
    for c in range(CHUNKS):
        keys += [("sibling", c), ("next", c, 0), ("next", c, 1)]
        for d in range(1, half):
            keys += [("y", c, d, 0), ("y", c, d, 1), ("relay", c, d, 0), ("relay", c, d, 1)]
    for s in range(len(SETS)):
        for d in range(1, half):
            keys += [("sum", s, d, 0), ("sum", s, d, 1), ("scale", s, d, 0), ("scale", s, d, 1)]
    return {key: i for i, key in enumerate(keys)}


def kernel(dims, amp, integ, lists_hbm, count, out, *scratch):
    groups, n, tiles, slots, rows_all, width = dims
    half = n // 2
    places = 2 * slots // n + tiles
    pairs = places // 2
    every_slot = 2 * slots
    group_targets = n * tiles
    rows_core = rows_all // 2
    rows = rows_core // CHUNKS
    wide = tiles * width
    group_tiles = n * tiles
    index = messages(half)
    gath = scratch[:CHUNKS]
    (vbuf, weights, mine, psend, precv, qsend, qrecv, ssend, srecv, lists, count_sib, following, walk, source, second,
     local_sem, send_sem, recv_sem) = scratch[CHUNKS:]

    g = lax.axis_index("task")
    me = lax.axis_index("own")
    core = lax.rem(me, 2)
    y = lax.div(me, 2)
    other = 1 - core
    next_g = lax.rem(g + 1, groups)
    prev_g = lax.rem(g + groups - 1, groups)
    sibling = y * 2 + other

    def ahead(d):
        return lax.rem(y + d, half)

    def behind(d):
        return lax.rem(y + half - d, half)

    def device(owner, group=g):
        return {"task": group, "own": owner}

    list_copy = pltpu.make_async_copy(lists_hbm, lists.at[0], local_sem.at[CHUNKS])
    list_copy.start()
    barrier = pltpu.get_barrier_semaphore()
    senders = [me, sibling]
    if "d" in ROUTES:
        senders += [behind(d) * 2 + side for d in range(1, half) for side in (core, other)]
    for owner in senders:
        pl.semaphore_signal(barrier, inc=1, device_id=device(owner, prev_g), device_id_type=MESH)
    for d in range(1, half):
        for rel in (core, other):
            pl.semaphore_signal(barrier, inc=1, device_id=device(ahead(d) * 2 + rel), device_id_type=MESH)
    pl.semaphore_signal(barrier, inc=1, device_id=device(sibling), device_id_type=MESH)
    v_copy = pltpu.make_async_copy(integ, vbuf.at[pl.ds(0, slots)], local_sem.at[CHUNKS + 1])
    v_copy.start()

    def own_rows(c, part):
        return amp.at[:, pl.ds(pl.multiple_of(part * rows_core + c * rows, 16), rows), :]

    def slot(c, offset, owner, count=1):
        return gath[c].at[pl.ds((offset * n + owner) * tiles, count * tiles)]

    local = []
    for c in range(CHUNKS):
        copy = pltpu.make_async_copy(own_rows(c, core), slot(c, 0, me), local_sem.at[c])
        copy.start()
        local.append(copy)

    sends = []

    def remote(key, src, dst, target, shift=0):
        i = index[key] + shift
        copy = pltpu.make_async_remote_copy(
            src_ref=src, dst_ref=dst, send_sem=send_sem.at[i], recv_sem=recv_sem.at[i], device_id=target, device_id_type=MESH
        )
        copy.start()
        sends.append(copy)

    def arrived(key, dst):
        pltpu.make_async_copy(dst, dst, recv_sem.at[index[key]]).wait()

    pl.semaphore_wait(barrier, n - 1 + len(senders))

    for step in range(CHUNKS):
        for part in range(2):
            rel = lax.rem(core + part, 2)
            c = ORDER_NEXT[step]
            remote(("next", c, 0), own_rows(c, part), slot(c, 1, me), device(y * 2 + part, next_g), rel)
        for part in range(2):
            rel = lax.rem(core + part, 2)
            if ROUTES[c] == "d":
                for d in range(1, half):
                    remote(("relay", c, d, 0), own_rows(c, part), slot(c, 1, me), device(ahead(d) * 2 + part, next_g), rel)
        for part in range(2):
            rel = lax.rem(core + part, 2)
            c = ORDER_Y[step]
            for d in range(1, half):
                remote(("y", c, d, 0), own_rows(c, part), slot(c, 0, me), device(ahead(d) * 2 + part), rel)
        if step == 0:
            remote(("lists",), lists_hbm, lists.at[1], device(sibling))
            remote(("count",), count, count_sib, device(sibling))
            remote(("integrals",), integ, vbuf.at[pl.ds(slots, slots)], device(sibling))
    for c in range(CHUNKS):
        remote(("sibling", c), own_rows(c, other), slot(c, 0, me), device(sibling))

    list_copy.wait()
    arrived(("lists",), lists.at[1])
    arrived(("count",), count_sib)

    for t in range(group_targets):
        following[every_slot * group_targets + t] = every_slot

    def back(step, firsts):
        k = every_slot - 1 - step
        e = lax.div(k, slots)
        target = lists[e, 2, k - e * slots]
        fresh = []
        for t in range(group_targets):
            first = jnp.where(target == t, k, firsts[t])
            following[k * group_targets + t] = first
            fresh.append(first)
        return tuple(fresh)

    lax.fori_loop(0, every_slot, back, tuple(jnp.int32(every_slot) for _ in range(group_targets)), unroll=16)

    def along(p, heads):
        fresh = []
        for t in range(group_targets):
            k = following[heads[t] * group_targets + t]
            walk[t * places + p] = k
            fresh.append(jnp.minimum(k + 1, every_slot))
        return tuple(fresh)

    lax.fori_loop(0, places, along, tuple(jnp.int32(0) for _ in range(group_targets)), unroll=2)
    live_own, live_sib = count[0], count_sib[0]

    def weigh(o, carry):
        for p in range(places):
            front = walk[o * tiles * places + p]
            k = jnp.minimum(front, walk[(o * tiles + 1) * places + places - 1 - p])
            if p % 2 == 0:
                second[o * pairs + p // 2] = jnp.where(front == every_slot, 1, 0)
            held = jnp.minimum(k, every_slot - 1)
            e = lax.div(held, slots)
            within = held - e * slots
            keep = jnp.logical_and(k < every_slot, within < jnp.where(e == 0, live_own, live_sib))
            source[o * places + p] = lists[e, 0, within] * group_tiles + lists[e, 1, within]
            block = vbuf[held]
            weights[o, p * width:(p + 1) * width, :] = jnp.where(keep, block, jnp.zeros_like(block))
        return carry

    def product(chunks, o):
        sums = [jnp.zeros((rows * len(chunks), width), jnp.float32) for _ in range(tiles)]
        for j in range(pairs):
            left = source[o * places + 2 * j]
            right = source[o * places + 2 * j + 1]
            tall = [jnp.concatenate([gath[c][left], gath[c][right]], -1) for c in chunks]
            part = jnp.dot(
                jnp.concatenate(tall, 0) if len(tall) > 1 else tall[0],
                weights[o, 2 * j * width:2 * (j + 1) * width, :],
                preferred_element_type=jnp.float32,
            )
            back_tile = second[o * pairs + j] == 1
            sums[0] = sums[0] + jnp.where(back_tile, 0.0, part)
            sums[1] = sums[1] + jnp.where(back_tile, part, 0.0)
        return jnp.concatenate(sums, -1)

    def relay_next(c):
        for d in range(1, half):
            here = slot(c, 0, behind(d) * 2, 2)
            arrived(("y", c, d, 0), slot(c, 0, behind(d) * 2 + core))
            arrived(("y", c, d, 1), slot(c, 0, behind(d) * 2 + other))
            remote(("relay", c, d, 0), here, slot(c, 1, behind(d) * 2, 2), device(me, next_g))

    def relay_y(c):
        arrived(("next", c, 0), slot(c, 1, me))
        arrived(("next", c, 1), slot(c, 1, sibling))
        for d in range(1, half):
            here = slot(c, 1, y * 2, 2)
            remote(("relay", c, d, 0), here, here, device(ahead(d) * 2 + core))

    def gathered(c):
        local[c].wait()
        arrived(("sibling", c), slot(c, 0, sibling))
        if ROUTES[c] != "y":
            arrived(("next", c, 0), slot(c, 1, me))
            arrived(("next", c, 1), slot(c, 1, sibling))
        for d in range(1, half):
            if ROUTES[c] != "x":
                arrived(("y", c, d, 0), slot(c, 0, behind(d) * 2 + core))
                arrived(("y", c, d, 1), slot(c, 0, behind(d) * 2 + other))
            if ROUTES[c] == "d":
                arrived(("relay", c, d, 0), slot(c, 1, behind(d) * 2 + core))
                arrived(("relay", c, d, 1), slot(c, 1, behind(d) * 2 + other))
            else:
                arrived(("relay", c, d, 0), slot(c, 1, behind(d) * 2, 2))

    firsts_of = [rows * sum(len(chunks) for chunks in SETS[:s]) for s in range(len(SETS))]

    def send_sums(s):
        held = pl.ds(firsts_of[s], rows * len(SETS[s]))
        for d in range(1, half):
            for part in range(2):
                rel = lax.rem(core + part, 2)
                o = ahead(d) * 2 + part
                total = product(SETS[s], o)
                top = jnp.maximum(jnp.max(jnp.abs(total), axis=0, keepdims=True), TINY)
                qsend[d - 1, part, held] = jnp.round(total * (LEVELS / top)).astype(jnp.int32).astype(jnp.int16)
                ssend[s, d - 1, part] = top * (1.0 / LEVELS)
                remote(("scale", s, d, 0), ssend.at[s, d - 1, part], srecv.at[s, d - 1, rel], device(o), rel)
                remote(("sum", s, d, 0), qsend.at[d - 1, part, held], qrecv.at[d - 1, rel, held], device(o), rel)

    def finish(s, rel):
        for d in range(1, half):
            arrived(("scale", s, d, rel), srecv.at[s, d - 1, rel])
            arrived(("sum", s, d, rel), qrecv.at[d - 1, rel, pl.ds(firsts_of[s], rows * len(SETS[s]))])
        for i, c in enumerate(SETS[s]):
            total = (mine if rel == 0 else precv)[pl.ds(c * rows, rows)]
            place = pl.ds(firsts_of[s] + i * rows, rows)
            for d in range(1, half):
                total = total + qrecv[d - 1, rel, place].astype(jnp.int32).astype(jnp.float32) * srecv[s, d - 1, rel]
            first = pl.multiple_of((core if rel == 0 else other) * rows_core + c * rows, 8)
            for t in range(tiles):
                out[t, pl.ds(first, rows), :] = total[:, t * width:(t + 1) * width]

    for c in ORDER_Y:
        if ROUTES[c] == "x":
            relay_next(c)
    v_copy.wait()
    arrived(("integrals",), vbuf.at[pl.ds(slots, slots)])
    lax.fori_loop(0, n, weigh, 0)
    for c in ORDER_NEXT:
        if ROUTES[c] == "y":
            relay_y(c)
    for s in range(len(SETS)):
        for c in SETS[s]:
            gathered(c)
        send_sums(s)
    every = list(range(CHUNKS))
    psend[...] = product(every, sibling)
    remote(("partial",), psend, precv, device(sibling))
    mine[...] = product(every, me)
    for s in range(len(SETS)):
        finish(s, 0)
    arrived(("partial",), precv)
    for s in range(len(SETS)):
        finish(s, 1)
    for copy in sends:
        copy.wait_send()


def shards(amplitudes, integrals, task_tiles, task_count):
    tiles, rows_all, width = amplitudes.shape
    slots = integrals.shape[0]
    groups, n = lax.axis_size("task"), lax.axis_size("own")
    half = n // 2
    peers = half - 1
    rows_core = rows_all // 2
    rows = rows_core // CHUNKS
    wide = tiles * width
    assert tiles == 2
    places = 2 * slots // n + tiles
    total = len(messages(half))
    dma = pltpu.SemaphoreType.DMA
    scratch = [pltpu.VMEM((2 * n * tiles, rows, width), amplitudes.dtype) for _ in range(CHUNKS)]
    scratch += [
        pltpu.VMEM((2 * slots, width, width), integrals.dtype),
        pltpu.VMEM((n, places * width, width), integrals.dtype),
        pltpu.VMEM((rows_core, wide), jnp.float32),
        pltpu.VMEM((rows_core, wide), jnp.float32),
        pltpu.VMEM((rows_core, wide), jnp.float32),
        pltpu.VMEM((peers, 2, rows_core, wide), jnp.int16),
        pltpu.VMEM((peers, 2, rows_core, wide), jnp.int16),
        pltpu.VMEM((len(SETS), peers, 2, 1, wide), jnp.float32),
        pltpu.VMEM((len(SETS), peers, 2, 1, wide), jnp.float32),
        pltpu.SMEM((2, 3, slots), jnp.int32),
        pltpu.SMEM((1,), jnp.int32),
        pltpu.SMEM(((2 * slots + 1) * n * tiles,), jnp.int32),
        pltpu.SMEM((n * tiles * places,), jnp.int32),
        pltpu.SMEM((n * places,), jnp.int32),
        pltpu.SMEM((n * places // 2,), jnp.int32),
        dma((CHUNKS + 2,)),
        dma((total,)),
        dma((total,)),
    ]
    dims = (groups, n, tiles, slots, rows_all, width)
    held = [pltpu.with_memory_space_constraint(x, pltpu.HBM) for x in (amplitudes, integrals, task_tiles.T)]
    return pl.pallas_call(
        functools.partial(kernel, dims),
        out_shape=pltpu.VMEM((tiles, rows_all, width), jnp.float32),
        in_specs=[
            pl.BlockSpec(memory_space=pl.ANY),
            pl.BlockSpec(memory_space=pl.ANY),
            pl.BlockSpec(memory_space=pl.ANY),
            pl.BlockSpec(memory_space=pltpu.SMEM),
        ],
        out_specs=pl.BlockSpec(memory_space=pltpu.VMEM),
        scratch_shapes=scratch,
        compiler_params=pltpu.CompilerParams(collective_id=0, has_side_effects=True, vmem_limit_bytes=VMEM_BYTES),
        name="ladder",
    )(*held, task_count)


def solution(mesh):
    return jax.shard_map(
        shards,
        mesh=mesh,
        in_specs=(
            P(("task", "own"), None, None),
            P(("task", "own"), None, None),
            P(("task", "own"), None),
            P(("task", "own")),
        ),
        out_specs=P(("task", "own"), None, None),
        check_vma=False,
    )
```

```python
import functools

import jax
import jax.numpy as jnp
from jax import lax
from jax.experimental import pallas as pl
from jax.experimental.pallas import tpu as pltpu
from jax.sharding import PartitionSpec as P

MESH = pl.DeviceIdType.MESH
CHUNKS = 6
SIZES = (1, 1, 1, 1, 1, 1)
UNITS = sum(SIZES)
ROUTES = "yyyyxx"
ORDER_Y = (4, 5, 0, 1, 2, 3)
ORDER_NEXT = (0, 1, 2, 3, 4, 5)
SETS = ((0,), (1, 4), (2, 3, 5))
LEVELS = 32767.0
TINY = 1e-33
VMEM_BYTES = 48 * 2**20


def messages(half):
    keys = [("integrals",), ("lists",), ("count",), ("partial",)]
    for c in range(CHUNKS):
        keys += [("sibling", c), ("next", c, 0), ("next", c, 1)]
        for d in range(1, half):
            keys += [("y", c, d, 0), ("y", c, d, 1), ("relay", c, d, 0), ("relay", c, d, 1)]
    for s in range(len(SETS)):
        for d in range(1, half):
            keys += [("sum", s, d, 0), ("sum", s, d, 1), ("scale", s, d, 0), ("scale", s, d, 1)]
    return {key: i for i, key in enumerate(keys)}


def kernel(dims, amp, integ, lists_hbm, count, out, *scratch):
    groups, n, tiles, slots, rows_all, width = dims
    half = n // 2
    places = 2 * slots // n + tiles
    pairs = places // 2
    every_slot = 2 * slots
    group_targets = n * tiles
    rows_core = rows_all // 2
    rows = [rows_core // UNITS * size for size in SIZES]
    start = [sum(rows[:c]) for c in range(CHUNKS)]
    wide = tiles * width
    group_tiles = n * tiles
    index = messages(half)
    gath = scratch[:CHUNKS]
    (stage, vbuf, weights, mine, psend, precv, qsend, qrecv, ssend, srecv, lists, count_sib, following, walk, source, second,
     local_sem, send_sem, recv_sem) = scratch[CHUNKS:]

    g = lax.axis_index("task")
    me = lax.axis_index("own")
    core = lax.rem(me, 2)
    y = lax.div(me, 2)
    other = 1 - core
    next_g = lax.rem(g + 1, groups)
    prev_g = lax.rem(g + groups - 1, groups)
    sibling = y * 2 + other

    def ahead(d):
        return lax.rem(y + d, half)

    def behind(d):
        return lax.rem(y + half - d, half)

    def device(owner, group=g):
        return {"task": group, "own": owner}

    list_copy = pltpu.make_async_copy(lists_hbm, lists.at[0], local_sem.at[CHUNKS])
    list_copy.start()
    stage_copy = pltpu.make_async_copy(amp, stage, local_sem.at[CHUNKS + 2])
    stage_copy.start()
    barrier = pltpu.get_barrier_semaphore()
    senders = [me, sibling]
    if "d" in ROUTES:
        senders += [behind(d) * 2 + side for d in range(1, half) for side in (core, other)]
    for owner in senders:
        pl.semaphore_signal(barrier, inc=1, device_id=device(owner, prev_g), device_id_type=MESH)
    for d in range(1, half):
        for rel in (core, other):
            pl.semaphore_signal(barrier, inc=1, device_id=device(ahead(d) * 2 + rel), device_id_type=MESH)
    pl.semaphore_signal(barrier, inc=1, device_id=device(sibling), device_id_type=MESH)
    v_copy = pltpu.make_async_copy(integ, vbuf.at[pl.ds(0, slots)], local_sem.at[CHUNKS + 1])
    v_copy.start()

    def own_rows(c, part, held=stage):
        return held.at[:, pl.ds(pl.multiple_of(part * rows_core + start[c], 16), rows[c]), :]

    def slot(c, offset, owner, count=1):
        return gath[c].at[pl.ds((offset * n + owner) * tiles, count * tiles)]

    local = []
    for c in range(CHUNKS):
        copy = pltpu.make_async_copy(own_rows(c, core, amp), slot(c, 0, me), local_sem.at[c])
        copy.start()
        local.append(copy)

    sends = []

    def remote(key, src, dst, target, shift=0):
        i = index[key] + shift
        copy = pltpu.make_async_remote_copy(
            src_ref=src, dst_ref=dst, send_sem=send_sem.at[i], recv_sem=recv_sem.at[i], device_id=target, device_id_type=MESH
        )
        copy.start()
        sends.append(copy)

    def arrived(key, dst):
        pltpu.make_async_copy(dst, dst, recv_sem.at[index[key]]).wait()

    stage_copy.wait()
    pl.semaphore_wait(barrier, n - 1 + len(senders))

    for i in range(CHUNKS):
        for part in range(2):
            rel = lax.rem(core + part, 2)
            c = ORDER_NEXT[i]
            remote(("next", c, 0), own_rows(c, part), slot(c, 1, me), device(y * 2 + part, next_g), rel)
        for part in range(2):
            rel = lax.rem(core + part, 2)
            c = ORDER_Y[i]
            for d in range(1, half):
                remote(("y", c, d, 0), own_rows(c, part), slot(c, 0, me), device(ahead(d) * 2 + part), rel)
        if i == 0:
            remote(("lists",), lists_hbm, lists.at[1], device(sibling))
            remote(("count",), count, count_sib, device(sibling))
            remote(("integrals",), integ, vbuf.at[pl.ds(slots, slots)], device(sibling))
    for c in range(CHUNKS):
        remote(("sibling", c), own_rows(c, other), slot(c, 0, me), device(sibling))

    list_copy.wait()
    arrived(("lists",), lists.at[1])
    arrived(("count",), count_sib)

    for t in range(group_targets):
        following[every_slot * group_targets + t] = every_slot

    def back(step, firsts):
        k = every_slot - 1 - step
        e = lax.div(k, slots)
        target = lists[e, 2, k - e * slots]
        fresh = []
        for t in range(group_targets):
            first = jnp.where(target == t, k, firsts[t])
            following[k * group_targets + t] = first
            fresh.append(first)
        return tuple(fresh)

    lax.fori_loop(0, every_slot, back, tuple(jnp.int32(every_slot) for _ in range(group_targets)), unroll=16)

    def along(p, heads):
        fresh = []
        for t in range(group_targets):
            k = following[heads[t] * group_targets + t]
            walk[t * places + p] = k
            fresh.append(jnp.minimum(k + 1, every_slot))
        return tuple(fresh)

    lax.fori_loop(0, places, along, tuple(jnp.int32(0) for _ in range(group_targets)), unroll=2)
    live_own, live_sib = count[0], count_sib[0]

    def weigh(o, carry):
        for p in range(places):
            front = walk[o * tiles * places + p]
            k = jnp.minimum(front, walk[(o * tiles + 1) * places + places - 1 - p])
            if p % 2 == 0:
                second[o * pairs + p // 2] = jnp.where(front == every_slot, 1, 0)
            held = jnp.minimum(k, every_slot - 1)
            e = lax.div(held, slots)
            within = held - e * slots
            keep = jnp.logical_and(k < every_slot, within < jnp.where(e == 0, live_own, live_sib))
            source[o * places + p] = lists[e, 0, within] * group_tiles + lists[e, 1, within]
            block = vbuf[held]
            weights[o, p * width:(p + 1) * width, :] = jnp.where(keep, block, jnp.zeros_like(block))
        return carry

    def product(chunks, o):
        sums = [jnp.zeros((sum(rows[c] for c in chunks), width), jnp.float32) for _ in range(tiles)]
        for j in range(pairs):
            left = source[o * places + 2 * j]
            right = source[o * places + 2 * j + 1]
            tall = [jnp.concatenate([gath[c][left], gath[c][right]], -1) for c in chunks]
            part = jnp.dot(
                jnp.concatenate(tall, 0) if len(tall) > 1 else tall[0],
                weights[o, 2 * j * width:2 * (j + 1) * width, :],
                preferred_element_type=jnp.float32,
            )
            back_tile = second[o * pairs + j] == 1
            sums[0] = sums[0] + jnp.where(back_tile, 0.0, part)
            sums[1] = sums[1] + jnp.where(back_tile, part, 0.0)
        return jnp.concatenate(sums, -1)

    def relay_next(c):
        for d in range(1, half):
            here = slot(c, 0, behind(d) * 2, 2)
            arrived(("y", c, d, 0), slot(c, 0, behind(d) * 2 + core))
            arrived(("y", c, d, 1), slot(c, 0, behind(d) * 2 + other))
            remote(("relay", c, d, 0), here, slot(c, 1, behind(d) * 2, 2), device(me, next_g))

    def relay_y(c):
        arrived(("next", c, 0), slot(c, 1, me))
        arrived(("next", c, 1), slot(c, 1, sibling))
        for d in range(1, half):
            here = slot(c, 1, y * 2, 2)
            remote(("relay", c, d, 0), here, here, device(ahead(d) * 2 + core))

    def gathered(c):
        local[c].wait()
        arrived(("sibling", c), slot(c, 0, sibling))
        if ROUTES[c] != "y":
            arrived(("next", c, 0), slot(c, 1, me))
            arrived(("next", c, 1), slot(c, 1, sibling))
        for d in range(1, half):
            if ROUTES[c] != "x":
                arrived(("y", c, d, 0), slot(c, 0, behind(d) * 2 + core))
                arrived(("y", c, d, 1), slot(c, 0, behind(d) * 2 + other))
            if ROUTES[c] == "d":
                arrived(("relay", c, d, 0), slot(c, 1, behind(d) * 2 + core))
                arrived(("relay", c, d, 1), slot(c, 1, behind(d) * 2 + other))
            else:
                arrived(("relay", c, d, 0), slot(c, 1, behind(d) * 2, 2))

    tall_of = [sum(rows[c] for c in chunks) for chunks in SETS]
    firsts_of = [sum(tall_of[:s]) for s in range(len(SETS))]

    def send_sums(s):
        held = pl.ds(firsts_of[s], tall_of[s])
        for d in range(1, half):
            for part in range(2):
                rel = lax.rem(core + part, 2)
                o = ahead(d) * 2 + part
                total = product(SETS[s], o)
                top = jnp.maximum(jnp.max(jnp.abs(total), axis=0, keepdims=True), TINY)
                qsend[d - 1, part, held] = jnp.round(total * (LEVELS / top)).astype(jnp.int32).astype(jnp.int16)
                ssend[s, d - 1, part] = top * (1.0 / LEVELS)
                remote(("scale", s, d, 0), ssend.at[s, d - 1, part], srecv.at[s, d - 1, rel], device(o), rel)
                remote(("sum", s, d, 0), qsend.at[d - 1, part, held], qrecv.at[d - 1, rel, held], device(o), rel)

    def finish(s, rel):
        for d in range(1, half):
            arrived(("scale", s, d, rel), srecv.at[s, d - 1, rel])
            arrived(("sum", s, d, rel), qrecv.at[d - 1, rel, pl.ds(firsts_of[s], tall_of[s])])
        for i, c in enumerate(SETS[s]):
            total = (mine if rel == 0 else precv)[pl.ds(start[c], rows[c])]
            place = pl.ds(firsts_of[s] + sum(rows[x] for x in SETS[s][:i]), rows[c])
            for d in range(1, half):
                total = total + qrecv[d - 1, rel, place].astype(jnp.int32).astype(jnp.float32) * srecv[s, d - 1, rel]
            first = pl.multiple_of((core if rel == 0 else other) * rows_core + start[c], 8)
            for t in range(tiles):
                out[t, pl.ds(first, rows[c]), :] = total[:, t * width:(t + 1) * width]

    for c in ORDER_Y:
        if ROUTES[c] == "x":
            relay_next(c)
    v_copy.wait()
    arrived(("integrals",), vbuf.at[pl.ds(slots, slots)])
    lax.fori_loop(0, n, weigh, 0)
    for c in ORDER_NEXT:
        if ROUTES[c] == "y":
            relay_y(c)
    for s in range(len(SETS)):
        for c in SETS[s]:
            gathered(c)
        send_sums(s)
    every = list(range(CHUNKS))
    psend[...] = product(every, sibling)
    remote(("partial",), psend, precv, device(sibling))
    mine[...] = product(every, me)
    arrived(("partial",), precv)
    for s in range(len(SETS)):
        finish(s, 0)
        finish(s, 1)
    for copy in sends:
        copy.wait_send()


def shards(amplitudes, integrals, task_tiles, task_count):
    tiles, rows_all, width = amplitudes.shape
    slots = integrals.shape[0]
    groups, n = lax.axis_size("task"), lax.axis_size("own")
    half = n // 2
    peers = half - 1
    rows_core = rows_all // 2
    wide = tiles * width
    assert tiles == 2
    places = 2 * slots // n + tiles
    total = len(messages(half))
    dma = pltpu.SemaphoreType.DMA
    scratch = [pltpu.VMEM((2 * n * tiles, rows_core // UNITS * size, width), amplitudes.dtype) for size in SIZES]
    scratch += [
        pltpu.VMEM(amplitudes.shape, amplitudes.dtype),
        pltpu.VMEM((2 * slots, width, width), integrals.dtype),
        pltpu.VMEM((n, places * width, width), integrals.dtype),
        pltpu.VMEM((rows_core, wide), jnp.float32),
        pltpu.VMEM((rows_core, wide), jnp.float32),
        pltpu.VMEM((rows_core, wide), jnp.float32),
        pltpu.VMEM((peers, 2, rows_core, wide), jnp.int16),
        pltpu.VMEM((peers, 2, rows_core, wide), jnp.int16),
        pltpu.VMEM((len(SETS), peers, 2, 1, wide), jnp.float32),
        pltpu.VMEM((len(SETS), peers, 2, 1, wide), jnp.float32),
        pltpu.SMEM((2, 3, slots), jnp.int32),
        pltpu.SMEM((1,), jnp.int32),
        pltpu.SMEM(((2 * slots + 1) * n * tiles,), jnp.int32),
        pltpu.SMEM((n * tiles * places,), jnp.int32),
        pltpu.SMEM((n * places,), jnp.int32),
        pltpu.SMEM((n * places // 2,), jnp.int32),
        dma((CHUNKS + 3,)),
        dma((total,)),
        dma((total,)),
    ]
    dims = (groups, n, tiles, slots, rows_all, width)
    held = [pltpu.with_memory_space_constraint(x, pltpu.HBM) for x in (amplitudes, integrals, task_tiles.T)]
    return pl.pallas_call(
        functools.partial(kernel, dims),
        out_shape=pltpu.VMEM((tiles, rows_all, width), jnp.float32),
        in_specs=[
            pl.BlockSpec(memory_space=pl.ANY),
            pl.BlockSpec(memory_space=pl.ANY),
            pl.BlockSpec(memory_space=pl.ANY),
            pl.BlockSpec(memory_space=pltpu.SMEM),
        ],
        out_specs=pl.BlockSpec(memory_space=pltpu.VMEM),
        scratch_shapes=scratch,
        compiler_params=pltpu.CompilerParams(collective_id=0, has_side_effects=True, vmem_limit_bytes=VMEM_BYTES),
        name="ladder",
    )(*held, task_count)


def solution(mesh):
    return jax.shard_map(
        shards,
        mesh=mesh,
        in_specs=(
            P(("task", "own"), None, None),
            P(("task", "own"), None, None),
            P(("task", "own"), None),
            P(("task", "own")),
        ),
        out_specs=P(("task", "own"), None, None),
        check_vma=False,
    )
```

```python
import functools

import jax
import jax.numpy as jnp
from jax import lax
from jax.experimental import pallas as pl
from jax.experimental.pallas import tpu as pltpu
from jax.sharding import PartitionSpec as P

MESH = pl.DeviceIdType.MESH
CHUNKS = 6
SIZES = (1, 1, 1, 1, 1, 1)
UNITS = sum(SIZES)
ROUTES = "yyyyxx"
ORDER_Y = (4, 5, 0, 1, 2, 3)
ORDER_NEXT = (0, 1, 2, 3, 4, 5)
SETS = ((0,), (1, 4), (2, 3, 5))
LEVELS = 32767.0
TINY = 1e-33
VMEM_BYTES = 48 * 2**20


def messages(half):
    keys = [("integrals",), ("lists",), ("count",), ("partial",)]
    for c in range(CHUNKS):
        keys += [("sibling", c), ("next", c, 0), ("next", c, 1)]
        for d in range(1, half):
            keys += [("y", c, d, 0), ("y", c, d, 1), ("relay", c, d, 0), ("relay", c, d, 1)]
    for s in range(len(SETS)):
        for d in range(1, half):
            keys += [("sum", s, d, 0), ("sum", s, d, 1), ("scale", s, d, 0), ("scale", s, d, 1)]
    return {key: i for i, key in enumerate(keys)}


def kernel(dims, amp, integ, lists_hbm, count, out, *scratch):
    groups, n, tiles, slots, rows_all, width = dims
    half = n // 2
    places = 2 * slots // n + tiles
    pairs = places // 2
    every_slot = 2 * slots
    group_targets = n * tiles
    rows_core = rows_all // 2
    rows = [rows_core // UNITS * size for size in SIZES]
    start = [sum(rows[:c]) for c in range(CHUNKS)]
    wide = tiles * width
    group_tiles = n * tiles
    index = messages(half)
    gath = scratch[:CHUNKS]
    (stage, vbuf, weights, mine, psend, precv, qsend, qrecv, ssend, srecv, lists, count_sib, following, walk, source, second,
     local_sem, send_sem, recv_sem) = scratch[CHUNKS:]

    g = lax.axis_index("task")
    me = lax.axis_index("own")
    core = lax.rem(me, 2)
    y = lax.div(me, 2)
    other = 1 - core
    kept = lax.rem(core + y, 2)
    next_g = lax.rem(g + 1, groups)
    prev_g = lax.rem(g + groups - 1, groups)
    sibling = y * 2 + other

    def ahead(d):
        return lax.rem(y + d, half)

    def behind(d):
        return lax.rem(y + half - d, half)

    def device(owner, group=g):
        return {"task": group, "own": owner}

    list_copy = pltpu.make_async_copy(lists_hbm, lists.at[0], local_sem.at[CHUNKS])
    list_copy.start()
    stage_copy = pltpu.make_async_copy(amp, stage, local_sem.at[CHUNKS + 2])
    stage_copy.start()
    barrier = pltpu.get_barrier_semaphore()
    senders = [me, sibling]
    if "d" in ROUTES:
        senders += [behind(d) * 2 + side for d in range(1, half) for side in (core, other)]
    for owner in senders:
        pl.semaphore_signal(barrier, inc=1, device_id=device(owner, prev_g), device_id_type=MESH)
    for d in range(1, half):
        for rel in (core, other):
            pl.semaphore_signal(barrier, inc=1, device_id=device(ahead(d) * 2 + rel), device_id_type=MESH)
    pl.semaphore_signal(barrier, inc=1, device_id=device(sibling), device_id_type=MESH)
    v_copy = pltpu.make_async_copy(integ, vbuf.at[pl.ds(0, slots)], local_sem.at[CHUNKS + 1])
    v_copy.start()

    def own_rows(c, part, held=stage):
        return held.at[:, pl.ds(pl.multiple_of(part * rows_core + start[c], 16), rows[c]), :]

    def slot(c, offset, owner, count=1):
        return gath[c].at[pl.ds((offset * n + owner) * tiles, count * tiles)]

    def holder(part, place):
        return lax.rem(part + place, 2)

    local = []
    for c in range(CHUNKS):
        copy = pltpu.make_async_copy(own_rows(c, kept, amp), slot(c, 0, me), local_sem.at[c])
        copy.start()
        local.append(copy)

    sends = []

    def remote(key, src, dst, target, shift=0):
        i = index[key] + shift
        copy = pltpu.make_async_remote_copy(
            src_ref=src, dst_ref=dst, send_sem=send_sem.at[i], recv_sem=recv_sem.at[i], device_id=target, device_id_type=MESH
        )
        copy.start()
        sends.append(copy)

    def arrived(key, dst):
        pltpu.make_async_copy(dst, dst, recv_sem.at[index[key]]).wait()

    stage_copy.wait()
    pl.semaphore_wait(barrier, n - 1 + len(senders))

    def send_next(i):
        c = ORDER_NEXT[i]
        for part in range(2):
            side = holder(part, y)
            remote(("next", c, 0), own_rows(c, part), slot(c, 1, me), device(y * 2 + side, next_g), lax.rem(core + side, 2))

    def send_y(i):
        c = ORDER_Y[i]
        for part in range(2):
            for d in range(1, half):
                side = holder(part, ahead(d))
                remote(("y", c, d, 0), own_rows(c, part), slot(c, 0, me), device(ahead(d) * 2 + side), lax.rem(core + side, 2))

    remote(("lists",), lists_hbm, lists.at[1], device(sibling))
    remote(("count",), count, count_sib, device(sibling))
    for i in range(CHUNKS):
        send_next(i)
        send_y(i)
        if i == 0:
            remote(("integrals",), integ, vbuf.at[pl.ds(slots, slots)], device(sibling))

    list_copy.wait()
    arrived(("lists",), lists.at[1])
    arrived(("count",), count_sib)

    for t in range(group_targets):
        following[every_slot * group_targets + t] = every_slot

    def back(step, firsts):
        k = every_slot - 1 - step
        e = lax.div(k, slots)
        target = lists[e, 2, k - e * slots]
        fresh = []
        for t in range(group_targets):
            first = jnp.where(target == t, k, firsts[t])
            following[k * group_targets + t] = first
            fresh.append(first)
        return tuple(fresh)

    lax.fori_loop(0, every_slot, back, tuple(jnp.int32(every_slot) for _ in range(group_targets)), unroll=16)

    def along(p, heads):
        fresh = []
        for t in range(group_targets):
            k = following[heads[t] * group_targets + t]
            walk[t * places + p] = k
            fresh.append(jnp.minimum(k + 1, every_slot))
        return tuple(fresh)

    lax.fori_loop(0, places, along, tuple(jnp.int32(0) for _ in range(group_targets)), unroll=2)
    live_own, live_sib = count[0], count_sib[0]

    def weigh(o, carry):
        for p in range(places):
            front = walk[o * tiles * places + p]
            k = jnp.minimum(front, walk[(o * tiles + 1) * places + places - 1 - p])
            if p % 2 == 0:
                second[o * pairs + p // 2] = jnp.where(front == every_slot, 1, 0)
            held = jnp.minimum(k, every_slot - 1)
            e = lax.div(held, slots)
            within = held - e * slots
            keep = jnp.logical_and(k < every_slot, within < jnp.where(e == 0, live_own, live_sib))
            source[o * places + p] = lists[e, 0, within] * group_tiles + lists[e, 1, within]
            block = vbuf[held]
            weights[o, p * width:(p + 1) * width, :] = jnp.where(keep, block, jnp.zeros_like(block))
        return carry

    def product(chunks, o):
        sums = [jnp.zeros((sum(rows[c] for c in chunks), width), jnp.float32) for _ in range(tiles)]
        for j in range(pairs):
            left = source[o * places + 2 * j]
            right = source[o * places + 2 * j + 1]
            tall = [jnp.concatenate([gath[c][left], gath[c][right]], -1) for c in chunks]
            part = jnp.dot(
                jnp.concatenate(tall, 0) if len(tall) > 1 else tall[0],
                weights[o, 2 * j * width:2 * (j + 1) * width, :],
                preferred_element_type=jnp.float32,
            )
            back_tile = second[o * pairs + j] == 1
            sums[0] = sums[0] + jnp.where(back_tile, 0.0, part)
            sums[1] = sums[1] + jnp.where(back_tile, part, 0.0)
        return jnp.concatenate(sums, -1)

    def relay_next(c):
        for d in range(1, half):
            here = slot(c, 0, behind(d) * 2, 2)
            arrived(("y", c, d, 0), slot(c, 0, behind(d) * 2 + core))
            arrived(("y", c, d, 1), slot(c, 0, behind(d) * 2 + other))
            remote(("relay", c, d, 0), here, slot(c, 1, behind(d) * 2, 2), device(me, next_g))

    def relay_y(c):
        arrived(("next", c, 0), slot(c, 1, me))
        arrived(("next", c, 1), slot(c, 1, sibling))
        for d in range(1, half):
            here = slot(c, 1, y * 2, 2)
            remote(("relay", c, d, 0), here, here, device(ahead(d) * 2 + holder(kept, ahead(d))))

    def gathered(c):
        local[c].wait()
        arrived(("sibling", c), slot(c, 0, sibling))
        if ROUTES[c] != "y":
            arrived(("next", c, 0), slot(c, 1, me))
            arrived(("next", c, 1), slot(c, 1, sibling))
        for d in range(1, half):
            if ROUTES[c] != "x":
                arrived(("y", c, d, 0), slot(c, 0, behind(d) * 2 + core))
                arrived(("y", c, d, 1), slot(c, 0, behind(d) * 2 + other))
            if ROUTES[c] == "d":
                arrived(("relay", c, d, 0), slot(c, 1, behind(d) * 2 + core))
                arrived(("relay", c, d, 1), slot(c, 1, behind(d) * 2 + other))
            else:
                arrived(("relay", c, d, 0), slot(c, 1, behind(d) * 2, 2))

    tall_of = [sum(rows[c] for c in chunks) for chunks in SETS]
    firsts_of = [sum(tall_of[:s]) for s in range(len(SETS))]

    def send_sums(s):
        held = pl.ds(firsts_of[s], tall_of[s])
        for d in range(1, half):
            for part in range(2):
                rel = lax.rem(core + part, 2)
                o = ahead(d) * 2 + part
                total = product(SETS[s], o)
                top = jnp.maximum(jnp.max(jnp.abs(total), axis=0, keepdims=True), TINY)
                qsend[d - 1, part, held] = jnp.round(total * (LEVELS / top)).astype(jnp.int32).astype(jnp.int16)
                ssend[s, d - 1, part] = top * (1.0 / LEVELS)
                remote(("scale", s, d, 0), ssend.at[s, d - 1, part], srecv.at[s, d - 1, rel], device(o), rel)
                remote(("sum", s, d, 0), qsend.at[d - 1, part, held], qrecv.at[d - 1, rel, held], device(o), rel)

    def finish(s, swap):
        for d in range(1, half):
            rel = (d + swap) % 2
            arrived(("scale", s, d, rel), srecv.at[s, d - 1, rel])
            arrived(("sum", s, d, rel), qrecv.at[d - 1, rel, pl.ds(firsts_of[s], tall_of[s])])
        for i, c in enumerate(SETS[s]):
            total = (mine if swap == 0 else precv)[pl.ds(start[c], rows[c])]
            place = pl.ds(firsts_of[s] + sum(rows[x] for x in SETS[s][:i]), rows[c])
            for d in range(1, half):
                rel = (d + swap) % 2
                total = total + qrecv[d - 1, rel, place].astype(jnp.int32).astype(jnp.float32) * srecv[s, d - 1, rel]
            first = pl.multiple_of((kept if swap == 0 else 1 - kept) * rows_core + start[c], 8)
            for t in range(tiles):
                out[t, pl.ds(first, rows[c]), :] = total[:, t * width:(t + 1) * width]

    for c in ORDER_Y:
        if ROUTES[c] == "x":
            relay_next(c)
    for c in range(CHUNKS):
        remote(("sibling", c), own_rows(c, 1 - kept), slot(c, 0, me), device(sibling))
    v_copy.wait()
    arrived(("integrals",), vbuf.at[pl.ds(slots, slots)])
    lax.fori_loop(0, n, weigh, 0)
    for c in ORDER_NEXT:
        if ROUTES[c] == "y":
            relay_y(c)
    for s in range(len(SETS)):
        for c in SETS[s]:
            gathered(c)
        send_sums(s)
    every = list(range(CHUNKS))
    psend[...] = product(every, sibling)
    remote(("partial",), psend, precv, device(sibling))
    mine[...] = product(every, me)
    arrived(("partial",), precv)
    for s in range(len(SETS)):
        finish(s, 0)
        finish(s, 1)
    for copy in sends:
        copy.wait_send()


def shards(amplitudes, integrals, task_tiles, task_count):
    tiles, rows_all, width = amplitudes.shape
    slots = integrals.shape[0]
    groups, n = lax.axis_size("task"), lax.axis_size("own")
    half = n // 2
    peers = half - 1
    rows_core = rows_all // 2
    wide = tiles * width
    assert tiles == 2
    places = 2 * slots // n + tiles
    total = len(messages(half))
    dma = pltpu.SemaphoreType.DMA
    scratch = [pltpu.VMEM((2 * n * tiles, rows_core // UNITS * size, width), amplitudes.dtype) for size in SIZES]
    scratch += [
        pltpu.VMEM(amplitudes.shape, amplitudes.dtype),
        pltpu.VMEM((2 * slots, width, width), integrals.dtype),
        pltpu.VMEM((n, places * width, width), integrals.dtype),
        pltpu.VMEM((rows_core, wide), jnp.float32),
        pltpu.VMEM((rows_core, wide), jnp.float32),
        pltpu.VMEM((rows_core, wide), jnp.float32),
        pltpu.VMEM((peers, 2, rows_core, wide), jnp.int16),
        pltpu.VMEM((peers, 2, rows_core, wide), jnp.int16),
        pltpu.VMEM((len(SETS), peers, 2, 1, wide), jnp.float32),
        pltpu.VMEM((len(SETS), peers, 2, 1, wide), jnp.float32),
        pltpu.SMEM((2, 3, slots), jnp.int32),
        pltpu.SMEM((1,), jnp.int32),
        pltpu.SMEM(((2 * slots + 1) * n * tiles,), jnp.int32),
        pltpu.SMEM((n * tiles * places,), jnp.int32),
        pltpu.SMEM((n * places,), jnp.int32),
        pltpu.SMEM((n * places // 2,), jnp.int32),
        dma((CHUNKS + 3,)),
        dma((total,)),
        dma((total,)),
    ]
    dims = (groups, n, tiles, slots, rows_all, width)
    held = [pltpu.with_memory_space_constraint(x, pltpu.HBM) for x in (amplitudes, integrals, task_tiles.T)]
    return pl.pallas_call(
        functools.partial(kernel, dims),
        out_shape=pltpu.VMEM((tiles, rows_all, width), jnp.float32),
        in_specs=[
            pl.BlockSpec(memory_space=pl.ANY),
            pl.BlockSpec(memory_space=pl.ANY),
            pl.BlockSpec(memory_space=pl.ANY),
            pl.BlockSpec(memory_space=pltpu.SMEM),
        ],
        out_specs=pl.BlockSpec(memory_space=pltpu.VMEM),
        scratch_shapes=scratch,
        compiler_params=pltpu.CompilerParams(collective_id=0, has_side_effects=True, vmem_limit_bytes=VMEM_BYTES),
        name="ladder",
    )(*held, task_count)


def solution(mesh):
    return jax.shard_map(
        shards,
        mesh=mesh,
        in_specs=(
            P(("task", "own"), None, None),
            P(("task", "own"), None, None),
            P(("task", "own"), None),
            P(("task", "own")),
        ),
        out_specs=P(("task", "own"), None, None),
        check_vma=False,
    )
```

```python
import functools

import jax
import jax.numpy as jnp
from jax import lax
from jax.experimental import pallas as pl
from jax.experimental.pallas import tpu as pltpu
from jax.sharding import PartitionSpec as P

MESH = pl.DeviceIdType.MESH
CHUNKS = 6
SIZES = (1, 1, 1, 1, 1, 1)
UNITS = sum(SIZES)
ROUTES = "yyyyxx"
ORDER_Y = (4, 5, 0, 1, 2, 3)
ORDER_NEXT = (0, 1, 2, 3, 4, 5)
SETS = ((0,), (1, 4), (2, 3, 5))
LEVELS = 32767.0
TINY = 1e-33
VMEM_BYTES = 48 * 2**20


def messages(half):
    keys = [("integrals",), ("lists",), ("count",), ("partial",)]
    for c in range(CHUNKS):
        keys += [("sibling", c), ("next", c, 0), ("next", c, 1)]
        for d in range(1, half):
            keys += [("y", c, d, 0), ("y", c, d, 1), ("relay", c, d, 0), ("relay", c, d, 1)]
    for s in range(len(SETS)):
        for d in range(1, half):
            keys += [("sum", s, d, 0), ("sum", s, d, 1), ("scale", s, d, 0), ("scale", s, d, 1)]
    return {key: i for i, key in enumerate(keys)}


def kernel(dims, amp, integ, lists_hbm, count, out, *scratch):
    groups, n, tiles, slots, rows_all, width = dims
    half = n // 2
    places = 2 * slots // n + tiles
    pairs = places // 2
    every_slot = 2 * slots
    group_targets = n * tiles
    rows_core = rows_all // 2
    rows = [rows_core // UNITS * size for size in SIZES]
    start = [sum(rows[:c]) for c in range(CHUNKS)]
    wide = tiles * width
    group_tiles = n * tiles
    index = messages(half)
    gath = scratch[:CHUNKS]
    (stage, vbuf, weights, mine, psend, precv, qsend, qrecv, ssend, srecv, lists, count_sib, following, walk, source, second,
     local_sem, send_sem, recv_sem) = scratch[CHUNKS:]

    g = lax.axis_index("task")
    me = lax.axis_index("own")
    core = lax.rem(me, 2)
    y = lax.div(me, 2)
    other = 1 - core
    kept = lax.rem(core + y, 2)
    next_g = lax.rem(g + 1, groups)
    prev_g = lax.rem(g + groups - 1, groups)
    sibling = y * 2 + other

    def ahead(d):
        return lax.rem(y + d, half)

    def behind(d):
        return lax.rem(y + half - d, half)

    def device(owner, group=g):
        return {"task": group, "own": owner}

    list_copy = pltpu.make_async_copy(lists_hbm, lists.at[0], local_sem.at[CHUNKS])
    list_copy.start()
    stage_copy = pltpu.make_async_copy(amp, stage, local_sem.at[CHUNKS + 2])
    stage_copy.start()
    barrier = pltpu.get_barrier_semaphore()
    senders = [me, sibling]
    if "d" in ROUTES:
        senders += [behind(d) * 2 + side for d in range(1, half) for side in (core, other)]
    for owner in senders:
        pl.semaphore_signal(barrier, inc=1, device_id=device(owner, prev_g), device_id_type=MESH)
    for d in range(1, half):
        for rel in (core, other):
            pl.semaphore_signal(barrier, inc=1, device_id=device(ahead(d) * 2 + rel), device_id_type=MESH)
    pl.semaphore_signal(barrier, inc=1, device_id=device(sibling), device_id_type=MESH)
    v_copy = pltpu.make_async_copy(integ, vbuf.at[pl.ds(0, slots)], local_sem.at[CHUNKS + 1])
    v_copy.start()

    def own_rows(c, part, held=stage):
        return held.at[:, pl.ds(pl.multiple_of(part * rows_core + start[c], 16), rows[c]), :]

    def slot(c, offset, owner, count=1):
        return gath[c].at[pl.ds((offset * n + owner) * tiles, count * tiles)]

    def holder(part, place):
        return lax.rem(part + place, 2)

    local = []
    for c in range(CHUNKS):
        copy = pltpu.make_async_copy(own_rows(c, kept, amp), slot(c, 0, me), local_sem.at[c])
        copy.start()
        local.append(copy)

    sends = []

    def remote(key, src, dst, target, shift=0):
        i = index[key] + shift
        copy = pltpu.make_async_remote_copy(
            src_ref=src, dst_ref=dst, send_sem=send_sem.at[i], recv_sem=recv_sem.at[i], device_id=target, device_id_type=MESH
        )
        copy.start()
        sends.append(copy)

    def arrived(key, dst):
        pltpu.make_async_copy(dst, dst, recv_sem.at[index[key]]).wait()

    stage_copy.wait()
    pl.semaphore_wait(barrier, n - 1 + len(senders))

    def send_next(i):
        c = ORDER_NEXT[i]
        for part in range(2):
            side = holder(part, y)
            remote(("next", c, 0), own_rows(c, part), slot(c, 1, me), device(y * 2 + side, next_g), lax.rem(core + side, 2))

    def send_y(i):
        c = ORDER_Y[i]
        for part in range(2):
            for d in range(1, half):
                side = holder(part, ahead(d))
                remote(("y", c, d, 0), own_rows(c, part), slot(c, 0, me), device(ahead(d) * 2 + side), lax.rem(core + side, 2))

    remote(("lists",), lists_hbm, lists.at[1], device(sibling))
    remote(("count",), count, count_sib, device(sibling))
    for i in range(CHUNKS):
        send_next(i)
        send_y(i)
        if i == 1:
            remote(("integrals",), integ, vbuf.at[pl.ds(slots, slots)], device(sibling))

    list_copy.wait()
    arrived(("lists",), lists.at[1])
    arrived(("count",), count_sib)

    for t in range(group_targets):
        following[every_slot * group_targets + t] = every_slot

    def back(step, firsts):
        k = every_slot - 1 - step
        e = lax.div(k, slots)
        target = lists[e, 2, k - e * slots]
        fresh = []
        for t in range(group_targets):
            first = jnp.where(target == t, k, firsts[t])
            following[k * group_targets + t] = first
            fresh.append(first)
        return tuple(fresh)

    lax.fori_loop(0, every_slot, back, tuple(jnp.int32(every_slot) for _ in range(group_targets)), unroll=16)

    def along(p, heads):
        fresh = []
        for t in range(group_targets):
            k = following[heads[t] * group_targets + t]
            walk[t * places + p] = k
            fresh.append(jnp.minimum(k + 1, every_slot))
        return tuple(fresh)

    lax.fori_loop(0, places, along, tuple(jnp.int32(0) for _ in range(group_targets)), unroll=2)
    live_own, live_sib = count[0], count_sib[0]

    def weigh(o, carry):
        for p in range(places):
            front = walk[o * tiles * places + p]
            k = jnp.minimum(front, walk[(o * tiles + 1) * places + places - 1 - p])
            if p % 2 == 0:
                second[o * pairs + p // 2] = jnp.where(front == every_slot, 1, 0)
            held = jnp.minimum(k, every_slot - 1)
            e = lax.div(held, slots)
            within = held - e * slots
            keep = jnp.logical_and(k < every_slot, within < jnp.where(e == 0, live_own, live_sib))
            source[o * places + p] = lists[e, 0, within] * group_tiles + lists[e, 1, within]
            block = vbuf[held]
            weights[o, p * width:(p + 1) * width, :] = jnp.where(keep, block, jnp.zeros_like(block))
        return carry

    def product(chunks, o):
        sums = [jnp.zeros((sum(rows[c] for c in chunks), width), jnp.float32) for _ in range(tiles)]
        for j in range(pairs):
            left = source[o * places + 2 * j]
            right = source[o * places + 2 * j + 1]
            tall = [jnp.concatenate([gath[c][left], gath[c][right]], -1) for c in chunks]
            part = jnp.dot(
                jnp.concatenate(tall, 0) if len(tall) > 1 else tall[0],
                weights[o, 2 * j * width:2 * (j + 1) * width, :],
                preferred_element_type=jnp.float32,
            )
            back_tile = second[o * pairs + j] == 1
            sums[0] = sums[0] + jnp.where(back_tile, 0.0, part)
            sums[1] = sums[1] + jnp.where(back_tile, part, 0.0)
        return jnp.concatenate(sums, -1)

    def relay_next(c):
        for d in range(1, half):
            here = slot(c, 0, behind(d) * 2, 2)
            arrived(("y", c, d, 0), slot(c, 0, behind(d) * 2 + core))
            arrived(("y", c, d, 1), slot(c, 0, behind(d) * 2 + other))
            remote(("relay", c, d, 0), here, slot(c, 1, behind(d) * 2, 2), device(me, next_g))

    def relay_y(c):
        arrived(("next", c, 0), slot(c, 1, me))
        arrived(("next", c, 1), slot(c, 1, sibling))
        for d in range(1, half):
            here = slot(c, 1, y * 2, 2)
            remote(("relay", c, d, 0), here, here, device(ahead(d) * 2 + holder(kept, ahead(d))))

    def gathered(c):
        local[c].wait()
        arrived(("sibling", c), slot(c, 0, sibling))
        if ROUTES[c] != "y":
            arrived(("next", c, 0), slot(c, 1, me))
            arrived(("next", c, 1), slot(c, 1, sibling))
        for d in range(1, half):
            if ROUTES[c] != "x":
                arrived(("y", c, d, 0), slot(c, 0, behind(d) * 2 + core))
                arrived(("y", c, d, 1), slot(c, 0, behind(d) * 2 + other))
            if ROUTES[c] == "d":
                arrived(("relay", c, d, 0), slot(c, 1, behind(d) * 2 + core))
                arrived(("relay", c, d, 1), slot(c, 1, behind(d) * 2 + other))
            else:
                arrived(("relay", c, d, 0), slot(c, 1, behind(d) * 2, 2))

    tall_of = [sum(rows[c] for c in chunks) for chunks in SETS]
    firsts_of = [sum(tall_of[:s]) for s in range(len(SETS))]

    def send_sums(s):
        held = pl.ds(firsts_of[s], tall_of[s])
        for d in range(1, half):
            for part in range(2):
                rel = lax.rem(core + part, 2)
                o = ahead(d) * 2 + part
                total = product(SETS[s], o)
                top = jnp.maximum(jnp.max(jnp.abs(total), axis=0, keepdims=True), TINY)
                qsend[d - 1, part, held] = jnp.round(total * (LEVELS / top)).astype(jnp.int32).astype(jnp.int16)
                ssend[s, d - 1, part] = top * (1.0 / LEVELS)
                remote(("scale", s, d, 0), ssend.at[s, d - 1, part], srecv.at[s, d - 1, rel], device(o), rel)
                remote(("sum", s, d, 0), qsend.at[d - 1, part, held], qrecv.at[d - 1, rel, held], device(o), rel)

    def finish(s, swap):
        for d in range(1, half):
            rel = (d + swap) % 2
            arrived(("scale", s, d, rel), srecv.at[s, d - 1, rel])
            arrived(("sum", s, d, rel), qrecv.at[d - 1, rel, pl.ds(firsts_of[s], tall_of[s])])
        for i, c in enumerate(SETS[s]):
            total = (mine if swap == 0 else precv)[pl.ds(start[c], rows[c])]
            place = pl.ds(firsts_of[s] + sum(rows[x] for x in SETS[s][:i]), rows[c])
            for d in range(1, half):
                rel = (d + swap) % 2
                total = total + qrecv[d - 1, rel, place].astype(jnp.int32).astype(jnp.float32) * srecv[s, d - 1, rel]
            first = pl.multiple_of((kept if swap == 0 else 1 - kept) * rows_core + start[c], 8)
            for t in range(tiles):
                out[t, pl.ds(first, rows[c]), :] = total[:, t * width:(t + 1) * width]

    for c in ORDER_Y:
        if ROUTES[c] == "x":
            relay_next(c)
    for c in range(CHUNKS):
        remote(("sibling", c), own_rows(c, 1 - kept), slot(c, 0, me), device(sibling))
    v_copy.wait()
    arrived(("integrals",), vbuf.at[pl.ds(slots, slots)])
    lax.fori_loop(0, n, weigh, 0)
    for c in ORDER_NEXT:
        if ROUTES[c] == "y":
            relay_y(c)
    for s in range(len(SETS)):
        for c in SETS[s]:
            gathered(c)
        send_sums(s)
    every = list(range(CHUNKS))
    psend[...] = product(every, sibling)
    remote(("partial",), psend, precv, device(sibling))
    mine[...] = product(every, me)
    arrived(("partial",), precv)
    for s in range(len(SETS)):
        finish(s, 0)
        finish(s, 1)
    for copy in sends:
        copy.wait_send()


def shards(amplitudes, integrals, task_tiles, task_count):
    tiles, rows_all, width = amplitudes.shape
    slots = integrals.shape[0]
    groups, n = lax.axis_size("task"), lax.axis_size("own")
    half = n // 2
    peers = half - 1
    rows_core = rows_all // 2
    wide = tiles * width
    assert tiles == 2
    places = 2 * slots // n + tiles
    total = len(messages(half))
    dma = pltpu.SemaphoreType.DMA
    scratch = [pltpu.VMEM((2 * n * tiles, rows_core // UNITS * size, width), amplitudes.dtype) for size in SIZES]
    scratch += [
        pltpu.VMEM(amplitudes.shape, amplitudes.dtype),
        pltpu.VMEM((2 * slots, width, width), integrals.dtype),
        pltpu.VMEM((n, places * width, width), integrals.dtype),
        pltpu.VMEM((rows_core, wide), jnp.float32),
        pltpu.VMEM((rows_core, wide), jnp.float32),
        pltpu.VMEM((rows_core, wide), jnp.float32),
        pltpu.VMEM((peers, 2, rows_core, wide), jnp.int16),
        pltpu.VMEM((peers, 2, rows_core, wide), jnp.int16),
        pltpu.VMEM((len(SETS), peers, 2, 1, wide), jnp.float32),
        pltpu.VMEM((len(SETS), peers, 2, 1, wide), jnp.float32),
        pltpu.SMEM((2, 3, slots), jnp.int32),
        pltpu.SMEM((1,), jnp.int32),
        pltpu.SMEM(((2 * slots + 1) * n * tiles,), jnp.int32),
        pltpu.SMEM((n * tiles * places,), jnp.int32),
        pltpu.SMEM((n * places,), jnp.int32),
        pltpu.SMEM((n * places // 2,), jnp.int32),
        dma((CHUNKS + 3,)),
        dma((total,)),
        dma((total,)),
    ]
    dims = (groups, n, tiles, slots, rows_all, width)
    held = [pltpu.with_memory_space_constraint(x, pltpu.HBM) for x in (amplitudes, integrals, task_tiles.T)]
    return pl.pallas_call(
        functools.partial(kernel, dims),
        out_shape=pltpu.VMEM((tiles, rows_all, width), jnp.float32),
        in_specs=[
            pl.BlockSpec(memory_space=pl.ANY),
            pl.BlockSpec(memory_space=pl.ANY),
            pl.BlockSpec(memory_space=pl.ANY),
            pl.BlockSpec(memory_space=pltpu.SMEM),
        ],
        out_specs=pl.BlockSpec(memory_space=pltpu.VMEM),
        scratch_shapes=scratch,
        compiler_params=pltpu.CompilerParams(collective_id=0, has_side_effects=True, vmem_limit_bytes=VMEM_BYTES),
        name="ladder",
    )(*held, task_count)


def solution(mesh):
    return jax.shard_map(
        shards,
        mesh=mesh,
        in_specs=(
            P(("task", "own"), None, None),
            P(("task", "own"), None, None),
            P(("task", "own"), None),
            P(("task", "own")),
        ),
        out_specs=P(("task", "own"), None, None),
        check_vma=False,
    )
```
